32 devices in a mesh: grp: 2 (over x), sub: 16 (over z, y, core).
Axes of the slice: x: 2, y: 2, z: 4, core: 2. Of those that a mesh axis runs over, the one named last changes fastest.
Arguments:
- resid: bfloat16 [2, 32, 2, 512, 256], P('grp', 'sub'), may hold values from -6 to 6
- kinv: bfloat16 [2, 32, 2, 512, 512], P('grp', 'sub'), may hold values from -2 to 2
- basis: bfloat16 [2, 32, 2, 8, 512], P('grp', 'sub'), may hold values from -2 to 2
- counts: int32 [2, 32], P('grp', 'sub'), may hold values from 1 to 8, as said below
- coarse_map: int32 [2, 32, 8], P('grp', 'sub'), may hold values from 0 to 127, as said below
- coarse_inv: float32 [2, 2, 128, 128], P('grp', None, 'sub'), may hold values from -1 to 1
Outputs:
- correction: bfloat16 [2, 32, 2, 512, 256], P('grp', 'sub')
The draws below stay inside these ranges and needn't reach their ends.
Inputs may be any that keep to these rules, and one draw needn't show every extreme that they name: `counts`: every draw has a subdomain with 8 live constraints. `coarse_map`: the constraints of subdomain j name coarse unknowns from 4 * j - 4 to 4 * j + 2 * 4 - 1, modulo 128; slots past the count hold values too.
All inputs are finite; a program needn't handle non-finite values.
Results may differ from the reference program's by a relative error of at most 0.0034.
Values may be sent and summed in bfloat16 or wider, within the bound.
A program may use at most 64 MiB of HBM per device.

```python
import jax
import jax.numpy as jnp
from jax import lax

ORDER = 512
IF = 64
PMAX = 8
CPS = 4
RHS = 256
NG = 2
NJ = 32
NC = 128


def draw_kinv(key, part):
    key_off, key_real, key_imag = jax.random.split(key, 3)
    shape = (NG, NJ, 2, ORDER, ORDER)
    off_diag = jax.random.normal(key_off, shape, jnp.float32) * (0.5 / ORDER ** 0.5)
    diag_real = jax.random.uniform(key_real, (NG, NJ, 1, ORDER), jnp.float32, 0.6, 1.4)
    diag_imag = jax.random.uniform(key_imag, (NG, NJ, 1, ORDER), jnp.float32, -0.4, 0.4)
    diagonal = jnp.concatenate([diag_real, diag_imag], axis=2)
    eye_rows = lax.broadcasted_iota(jnp.int32, (ORDER, ORDER), 0)
    eye_cols = lax.broadcasted_iota(jnp.int32, (ORDER, ORDER), 1)
    identity = (eye_rows == eye_cols).astype(jnp.float32)
    full = off_diag + identity * diagonal[..., :, None]
    return jnp.clip(full, -2.0, 2.0).astype(jnp.bfloat16)


def draw_coarse_inv(key, part):
    key_off, key_real, key_imag = jax.random.split(key, 3)
    shape = (NG, 2, NC, NC)
    off_diag = jax.random.normal(key_off, shape, jnp.float32) * (0.12 / NC ** 0.5)
    diag_real = jax.random.uniform(key_real, (NG, 1, NC), jnp.float32, 0.2, 0.4)
    diag_imag = jax.random.uniform(key_imag, (NG, 1, NC), jnp.float32, -0.1, 0.1)
    diagonal = jnp.concatenate([diag_real, diag_imag], axis=1)
    eye_rows = lax.broadcasted_iota(jnp.int32, (NC, NC), 0)
    eye_cols = lax.broadcasted_iota(jnp.int32, (NC, NC), 1)
    identity = (eye_rows == eye_cols).astype(jnp.float32)
    full = off_diag + identity * diagonal[..., :, None]
    return jnp.clip(full, -1.0, 1.0)


def draw_counts(key, part):
    key_vals, key_pos = jax.random.split(key)
    drawn = jax.random.randint(key_vals, (NG * NJ,), 1, PMAX + 1, jnp.int32)
    position = jax.random.randint(key_pos, (), 0, NG * NJ, jnp.int32)
    flat_ids = jnp.arange(NG * NJ, dtype=jnp.int32)
    drawn = jnp.where(flat_ids == position, PMAX, drawn)
    return drawn.reshape(NG, NJ)


def draw_coarse_map(key, part):
    offsets = jax.random.randint(key, (NG, NJ, PMAX), -CPS, 2 * CPS, jnp.int32)
    base_ids = (CPS * jnp.arange(NJ, dtype=jnp.int32))[None, :, None]
    mapped = (base_ids + offsets) % NC
    slot_ids = jnp.arange(PMAX, dtype=jnp.int32)[None, None, :]
    mapped = jnp.where(slot_ids == 0, base_ids + CPS - 1, mapped)
    mapped = jnp.where(slot_ids == 1, base_ids, mapped)
    return mapped.astype(jnp.int32)


def steps_of(rng, shape, cuts, least, top_value):
    gain = 1.0
    for dim, blocks in cuts:
        steps = jax.random.uniform(jax.random.fold_in(jax.random.fold_in(rng, 6), dim), (blocks,), jnp.float32, least / len(cuts), top_value / len(cuts))
        gain = gain * jnp.repeat(jnp.exp(steps), shape[dim] // blocks).reshape((-1,) + (1,) * (len(shape) - 1 - dim))
    return gain


def noise(rng, dims, scale, bound, shards=(), kind=jnp.bfloat16):
    level = steps_of(rng, dims, shards, -0.22, 0.18) if shards else 1.0
    values = jax.random.normal(rng, dims, jnp.float32) * scale * level
    return jnp.minimum(jnp.maximum(values, -bound), bound).astype(kind)


def setup_inputs(seed: int = 0) -> dict:
    seeds = jax.random.split(jax.random.key(seed), 7)
    return {
        "resid": noise(seeds[0], (NG, NJ, 2, ORDER, RHS), 1.0, 6.0, ((0, 2), (1, 16))),
        "kinv": draw_kinv(jax.random.fold_in(seeds[6], 71), 0),
        "basis": noise(seeds[2], (NG, NJ, 2, PMAX, ORDER), 0.15, 2.0, ((0, 2), (1, 16))),
        "counts": draw_counts(jax.random.fold_in(seeds[6], 71), 0),
        "coarse_map": draw_coarse_map(jax.random.fold_in(seeds[6], 71), 0),
        "coarse_inv": draw_coarse_inv(jax.random.fold_in(seeds[6], 71), 0),
    }


def complex_product(matrix, vector):
    parts = jnp.einsum("...cik,...dkr->...cdir", matrix.astype(jnp.float32), vector.astype(jnp.float32), precision=lax.Precision.HIGHEST)
    real_part = parts[..., 0, 0, :, :] - parts[..., 1, 1, :, :]
    imag_part = parts[..., 0, 1, :, :] + parts[..., 1, 0, :, :]
    return jnp.stack([real_part, imag_part], axis=-3)


def reference(resid, kinv, basis, counts, coarse_map, coarse_inv):
    values = resid.astype(jnp.float32)
    lefts = values[:, :, :, :IF]
    rights = values[:, :, :, IF:2 * IF]
    lowers = values[:, :, :, 2 * IF:3 * IF]
    uppers = values[:, :, :, 3 * IF:4 * IF]
    from_prev = jnp.roll(rights, 1, axis=1)
    from_next = jnp.roll(lefts, -1, axis=1)
    from_below = jnp.concatenate([jnp.zeros_like(uppers[:1]), uppers[:-1]], axis=0)
    from_above = jnp.concatenate([lowers[1:], jnp.zeros_like(lowers[:1])], axis=0)
    group_ids = jnp.arange(NG)[:, None, None, None, None]
    low_weight = jnp.where(group_ids > 0, 0.5, 1.0).astype(jnp.float32)
    high_weight = jnp.where(group_ids < NG - 1, 0.5, 1.0).astype(jnp.float32)
    weighted = jnp.concatenate([
        0.5 * lefts + 0.5 * from_prev,
        0.5 * rights + 0.5 * from_next,
        low_weight * lowers + 0.5 * from_below,
        high_weight * uppers + 0.5 * from_above,
        values[:, :, :, 4 * IF:]], axis=3).astype(jnp.bfloat16)

    def one_group(items):
        group_w, group_k, group_b, group_c, group_m, group_ci = items
        local = complex_product(group_k, group_w)
        primal = complex_product(group_b, group_w)
        slots = jnp.arange(PMAX)[None, :]
        live = (slots < group_c[:, None]).astype(jnp.float32)
        primal = primal * live[:, None, :, None]
        table = (group_m[:, :, None] == jnp.arange(NC)[None, None, :]).astype(jnp.float32) * live[:, :, None]
        rhs = jnp.einsum("jpn,jcpr->cnr", table, primal, precision=lax.Precision.HIGHEST)
        solved = complex_product(group_ci, rhs)
        picked = jnp.einsum("jpn,cnr->jcpr", table, solved, precision=lax.Precision.HIGHEST)
        spread = complex_product(jnp.swapaxes(group_b, 2, 3), picked)
        return (local + spread).astype(jnp.bfloat16)

    return lax.map(one_group, (weighted, kinv, basis, counts, coarse_map, coarse_inv))
```

```python
import functools

import jax
import jax.numpy as jnp
from jax import lax
from jax.experimental import pallas as pl
from jax.experimental.pallas import tpu as pltpu
from jax.sharding import PartitionSpec as P

IF = 64
CPS = 4
MESH = pl.DeviceIdType.MESH
F32 = jnp.float32
BF16 = jnp.bfloat16


def dot(a, b):
    return jnp.dot(a, b, preferred_element_type=F32)


def repeat(first, last, body):
    if last - first <= 8:
        for k in range(first, last):
            body(k)
    else:
        lax.fori_loop(first, last, lambda k, c: (body(k), c)[1], 0)


def split(x):
    high = x.astype(BF16)
    return high, (x - high.astype(F32)).astype(BF16)


def kernel(
    n, groups, resid, kinv, basis, counts, cmap, coarse, out,
    vals, kin, below, above, fprev, fnext, cprev, cnext, gather, wt, acc,
    load_sem, halo_send, halo_recv, ag_send, ag_recv,
):
    subs, _, order, width = vals.shape
    shared = 4 * IF
    rows_own, nc = coarse.shape[2], coarse.shape[3]
    rows_w = gather.shape[2]
    me = lax.axis_index("sub")
    grp = lax.axis_index("grp")
    nxt, prv = lax.rem(me + 1, n), lax.rem(me + n - 1, n)
    chips = n // 2
    chip, core = me // 2, lax.rem(me, 2)
    sib = chip * 2 + 1 - core
    has_below, has_above = grp > 0, grp < groups - 1

    barrier = pltpu.get_barrier_semaphore()

    def greet(k):
        pl.semaphore_signal(
            barrier, inc=1, device_id={"sub": lax.rem(me + k, n)}, device_id_type=MESH
        )

    @pl.when(has_above)
    def _():
        pl.semaphore_signal(barrier, inc=1, device_id={"grp": grp + 1}, device_id_type=MESH)

    @pl.when(has_below)
    def _():
        pl.semaphore_signal(barrier, inc=1, device_id={"grp": grp - 1}, device_id_type=MESH)

    if n <= 16:
        for k in range(1, n):
            greet(k)
    else:
        repeat(1, n, greet)

    load_vals = pltpu.make_async_copy(resid.at[0], vals, load_sem.at[0])
    load_kinv = pltpu.make_async_copy(kinv.at[0], kin, load_sem.at[1])
    load_vals.start()
    load_kinv.start()

    def push(i, src, dst, where):
        return pltpu.make_async_remote_copy(
            src_ref=src, dst_ref=dst, send_sem=halo_send.at[i], recv_sem=halo_recv.at[i],
            device_id=where, device_id_type=MESH,
        )

    to_next = push(0, resid.at[0, subs - 1, :, pl.ds(IF, IF)], fprev, {"sub": nxt})
    to_prev = push(1, resid.at[0, 0, :, pl.ds(0, IF)], fnext, {"sub": prv})
    to_above = push(2, resid.at[0, :, :, pl.ds(3 * IF, IF)], below, {"grp": grp + 1})
    to_below = push(3, resid.at[0, :, :, pl.ds(2 * IF, IF)], above, {"grp": grp - 1})
    c_next = push(4, coarse, cprev, {"sub": nxt})
    c_prev = push(5, coarse, cnext, {"sub": prv})

    pl.semaphore_wait(
        barrier, n - 1 + has_above.astype(jnp.int32) + has_below.astype(jnp.int32)
    )

    @pl.when(has_above)
    def _():
        to_above.start()

    @pl.when(has_below)
    def _():
        to_below.start()

    to_next.start()
    to_prev.start()
    c_next.start()
    c_prev.start()

    windowed = []
    for s in range(subs):
        relative = cmap[0, s : s + 1, :] - CPS * (me * subs + s) + CPS
        relative = jnp.where(relative < 0, relative + nc, relative)
        relative = jnp.where(relative >= nc, relative - nc, relative) + CPS * s
        pmax = relative.shape[1]
        spots = lax.broadcasted_iota(jnp.int32, (rows_w, pmax), 0)
        slots = lax.broadcasted_iota(jnp.int32, (rows_w, pmax), 1)
        hit = (spots == relative) & (slots < counts[:, s : s + 1])
        table = hit.astype(F32).astype(BF16)
        both = [dot(table, basis[0, s, c]) for c in range(2)]
        windowed.append(jnp.concatenate(both, axis=0))

    rows = lax.broadcasted_iota(jnp.int32, (nc, n * rows_w), 0)
    cols = lax.broadcasted_iota(jnp.int32, (nc, n * rows_w), 1)
    place = (cols // rows_w) * rows_own - CPS + lax.rem(cols, rows_w)
    place = jnp.where(place < 0, place + nc, place)
    place = jnp.where(place >= nc, place - nc, place)
    within = lax.rem(cols, rows_w) < rows_own + 2 * CPS
    pick = ((rows == place) & within).astype(F32).astype(BF16)

    load_vals.wait()
    load_kinv.wait()

    def combine(k_cols, real, imag):
        lhs = jnp.concatenate(k_cols, axis=1)
        rhs_real = jnp.concatenate([real, -imag], axis=0)
        rhs_imag = jnp.concatenate([imag, real], axis=0)
        return dot(lhs, rhs_real), dot(lhs, rhs_imag)

    def window_part(table, real, imag):
        high = table.astype(BF16)
        both_real, both_imag = dot(high, real), dot(high, imag)
        return (
            both_real[:rows_w] - both_imag[rows_w:],
            both_imag[:rows_w] + both_real[rows_w:],
        )

    w_real = jnp.zeros((rows_w, width), F32)
    w_imag = jnp.zeros((rows_w, width), F32)
    for s in range(subs):
        real, imag = vals[s, 0, shared:], vals[s, 1, shared:]
        part = window_part(windowed[s][:, shared:], real, imag)
        w_real, w_imag = w_real + part[0], w_imag + part[1]
        got = combine([kin[s, 0, :, shared:], kin[s, 1, :, shared:]], real, imag)
        acc[s, 0], acc[s, 1] = got

    to_next.wait_recv()
    to_prev.wait_recv()

    @pl.when(has_below)
    def _():
        to_above.wait_recv()

    @pl.when(has_above)
    def _():
        to_below.wait_recv()

    low = jnp.where(has_below, 0.5, 1.0).astype(F32)
    high = jnp.where(has_above, 0.5, 1.0).astype(F32)
    for s in range(subs):
        for c in range(2):
            own = [vals[s, c, IF * i : IF * (i + 1)].astype(F32) for i in range(4)]
            left = fprev[c] if s == 0 else vals[s - 1, c, IF : 2 * IF]
            right = fnext[c] if s == subs - 1 else vals[s + 1, c, 0:IF]
            zero = jnp.zeros((IF, width), F32)
            under = jnp.where(has_below, below[s, c].astype(F32), zero)
            over = jnp.where(has_above, above[s, c].astype(F32), zero)
            wt[s, c, 0:IF] = (0.5 * own[0] + 0.5 * left.astype(F32)).astype(BF16)
            wt[s, c, IF : 2 * IF] = (0.5 * own[1] + 0.5 * right.astype(F32)).astype(BF16)
            wt[s, c, 2 * IF : 3 * IF] = (low * own[2] + 0.5 * under).astype(BF16)
            wt[s, c, 3 * IF : 4 * IF] = (high * own[3] + 0.5 * over).astype(BF16)
        part = window_part(windowed[s][:, :shared], wt[s, 0], wt[s, 1])
        w_real, w_imag = w_real + part[0], w_imag + part[1]

    gather[me, 0] = w_real.astype(BF16)
    gather[me, 1] = w_imag.astype(BF16)

    def share(slot, where, i):
        return pltpu.make_async_remote_copy(
            src_ref=gather.at[slot], dst_ref=gather.at[slot],
            send_sem=ag_send.at[i], recv_sem=ag_recv.at[slot],
            device_id={"sub": where}, device_id_type=MESH,
        )

    def across(k):
        return share(me, lax.rem(chip + k, chips) * 2 + core, k)

    def source(k):
        return lax.rem(chip + chips - k, chips) * 2 + core

    def relay(k):
        return share(source(k), sib, chips + k)

    repeat(1, chips, lambda k: across(k).start())
    share(me, sib, 0).start()

    c_next.wait_recv()
    c_prev.wait_recv()
    pieces = []
    for c in range(2):
        parts = [cprev[0, c, rows_own - CPS :], coarse[0, c], cnext[0, c, :CPS]]
        extra = rows_w - rows_own - 2 * CPS
        if extra:
            parts.append(jnp.zeros((extra, nc), F32))
        pieces.extend(split(jnp.concatenate(parts, axis=0)))
    coarse_ext = dot(jnp.concatenate(pieces, axis=0), pick).astype(BF16)
    columns = [w.astype(BF16).T for w in windowed]

    def forward(k):
        share(source(k), sib, k).wait_recv()
        relay(k).start()

    for s in range(subs):
        got = combine([kin[s, 0, :, :shared], kin[s, 1, :, :shared]], wt[s, 0], wt[s, 1])
        acc[s, 0] += got[0]
        acc[s, 1] += got[1]

    repeat(1, chips, forward)
    repeat(0, chips, lambda k: share(lax.rem(chip + k, chips) * 2 + 1 - core, sib, 0).wait_recv())

    all_real = gather[:, 0].reshape(n * rows_w, width)
    all_imag = gather[:, 1].reshape(n * rows_w, width)
    by_real, by_imag = dot(coarse_ext, all_real), dot(coarse_ext, all_imag)

    def whole(x, i):
        return x[2 * i * rows_w : (2 * i + 1) * rows_w] + x[(2 * i + 1) * rows_w : (2 * i + 2) * rows_w]

    solved_real = whole(by_real, 0) - whole(by_imag, 1)
    solved_imag = whole(by_imag, 0) + whole(by_real, 1)
    real_high, real_low = split(solved_real)
    imag_high, imag_low = split(solved_imag)
    rhs_real = jnp.concatenate([real_high, -imag_high, real_low, -imag_low], axis=0)
    rhs_imag = jnp.concatenate([imag_high, real_high, imag_low, real_low], axis=0)
    for s in range(subs):
        lhs = jnp.concatenate([columns[s], columns[s]], axis=1)
        out[0, s, 0] = (acc[s, 0] + dot(lhs, rhs_real)).astype(BF16)
        out[0, s, 1] = (acc[s, 1] + dot(lhs, rhs_imag)).astype(BF16)

    to_next.wait_send()
    to_prev.wait_send()

    @pl.when(has_above)
    def _():
        to_above.wait_send()

    @pl.when(has_below)
    def _():
        to_below.wait_send()

    c_next.wait_send()
    c_prev.wait_send()
    share(me, sib, 0).wait_send()
    repeat(1, chips, lambda k: across(k).wait_send())
    repeat(1, chips, lambda k: relay(k).wait_send())


def per_device(n, groups, resid, kinv, basis, counts, coarse_map, coarse_inv):
    _, subs, _, order, width = resid.shape
    rows_w = -(-(CPS * (subs + 2)) // 16) * 16
    vmem = pl.BlockSpec(memory_space=pltpu.VMEM)
    hbm = pl.BlockSpec(memory_space=pl.ANY)
    dma = pltpu.SemaphoreType.DMA
    return pl.pallas_call(
        functools.partial(kernel, n, groups),
        out_shape=jax.ShapeDtypeStruct(resid.shape, BF16),
        in_specs=[hbm, hbm, vmem, vmem, vmem, vmem],
        out_specs=vmem,
        scratch_shapes=[
            pltpu.VMEM(resid.shape[1:], BF16),
            pltpu.VMEM(kinv.shape[1:], BF16),
            pltpu.VMEM((subs, 2, IF, width), BF16),
            pltpu.VMEM((subs, 2, IF, width), BF16),
            pltpu.VMEM((2, IF, width), BF16),
            pltpu.VMEM((2, IF, width), BF16),
            pltpu.VMEM(coarse_inv.shape, F32),
            pltpu.VMEM(coarse_inv.shape, F32),
            pltpu.VMEM((n, 2, rows_w, width), BF16),
            pltpu.VMEM((subs, 2, 4 * IF, width), BF16),
            pltpu.VMEM((subs, 2, order, width), F32),
            dma((2,)), dma((6,)), dma((6,)), dma((n,)), dma((n,)),
        ],
        compiler_params=pltpu.CompilerParams(collective_id=0, has_side_effects=True),
    )(resid, kinv, basis, counts, coarse_map, coarse_inv)


def solution(mesh):
    return jax.shard_map(
        functools.partial(per_device, mesh.shape["sub"], mesh.shape["grp"]),
        mesh=mesh,
        in_specs=(
            P("grp", "sub", None, None, None),
            P("grp", "sub", None, None, None),
            P("grp", "sub", None, None, None),
            P("grp", "sub"),
            P("grp", "sub", None),
            P("grp", None, "sub", None),
        ),
        out_specs=P("grp", "sub", None, None, None),
        check_vma=False,
    )
```

```python
import functools

import jax
import jax.numpy as jnp
from jax import lax
from jax.experimental import pallas as pl
from jax.experimental.pallas import tpu as pltpu
from jax.sharding import PartitionSpec as P

IF = 64
CPS = 4
MESH = pl.DeviceIdType.MESH
F32 = jnp.float32
BF16 = jnp.bfloat16


def dot(a, b):
    return jnp.dot(a, b, preferred_element_type=F32)


def repeat(first, last, body):
    if last - first <= 8:
        for k in range(first, last):
            body(k)
    else:
        lax.fori_loop(first, last, lambda k, c: (body(k), c)[1], 0)


def split(x):
    high = x.astype(BF16)
    return high, (x - high.astype(F32)).astype(BF16)


def kernel(
    n, groups, resid, kinv, basis_hbm, counts_hbm, cmap_hbm, coarse_hbm, out,
    basis, counts, cmap, coarse, vals, kin, below, above, fprev, fnext, cprev, cnext, gather, wt, acc,
    load_sem, halo_send, halo_recv, ag_send, ag_recv,
):
    subs, _, order, width = vals.shape
    shared = 4 * IF
    rows_own, nc = coarse.shape[2], coarse.shape[3]
    rows_w = gather.shape[2]
    me = lax.axis_index("sub")
    grp = lax.axis_index("grp")
    nxt, prv = lax.rem(me + 1, n), lax.rem(me + n - 1, n)
    chips = n // 2
    chip, core = me // 2, lax.rem(me, 2)
    sib = chip * 2 + 1 - core
    has_below, has_above = grp > 0, grp < groups - 1

    barrier = pltpu.get_barrier_semaphore()

    def greet(k):
        pl.semaphore_signal(
            barrier, inc=1, device_id={"sub": lax.rem(me + k, n)}, device_id_type=MESH
        )

    @pl.when(has_above)
    def _():
        pl.semaphore_signal(barrier, inc=1, device_id={"grp": grp + 1}, device_id_type=MESH)

    @pl.when(has_below)
    def _():
        pl.semaphore_signal(barrier, inc=1, device_id={"grp": grp - 1}, device_id_type=MESH)

    def greet_chip(k):
        pl.semaphore_signal(
            barrier, inc=1, device_id={"sub": lax.rem(chip + k, chips) * 2 + core}, device_id_type=MESH
        )

    repeat(1, chips, greet_chip)
    pl.semaphore_signal(barrier, inc=1, device_id={"sub": sib}, device_id_type=MESH)
    beyond = jnp.where(core == 1, nxt, prv)
    pl.semaphore_signal(barrier, inc=1, device_id={"sub": beyond}, device_id_type=MESH)

    load_vals = pltpu.make_async_copy(resid.at[0], vals, load_sem.at[0])
    load_kinv = pltpu.make_async_copy(kinv.at[0], kin, load_sem.at[1])
    small = [
        pltpu.make_async_copy(src, dst, load_sem.at[2 + i])
        for i, (src, dst) in enumerate(
            [(coarse_hbm, coarse), (cmap_hbm, cmap), (counts_hbm, counts), (basis_hbm, basis)]
        )
    ]
    for load in small:
        load.start()
    load_vals.start()
    load_kinv.start()

    def push(i, src, dst, where):
        return pltpu.make_async_remote_copy(
            src_ref=src, dst_ref=dst, send_sem=halo_send.at[i], recv_sem=halo_recv.at[i],
            device_id=where, device_id_type=MESH,
        )

    to_next = push(0, resid.at[0, subs - 1, :, pl.ds(IF, IF)], fprev, {"sub": nxt})
    to_prev = push(1, resid.at[0, 0, :, pl.ds(0, IF)], fnext, {"sub": prv})
    to_above = push(2, resid.at[0, :, :, pl.ds(3 * IF, IF)], below, {"grp": grp + 1})
    to_below = push(3, resid.at[0, :, :, pl.ds(2 * IF, IF)], above, {"grp": grp - 1})
    c_next = push(4, coarse, cprev, {"sub": nxt})
    c_prev = push(5, coarse, cnext, {"sub": prv})

    for load in small:
        load.wait()
    pl.semaphore_wait(
        barrier, chips + 1 + has_above.astype(jnp.int32) + has_below.astype(jnp.int32)
    )

    @pl.when(has_above)
    def _():
        to_above.start()

    @pl.when(has_below)
    def _():
        to_below.start()

    to_next.start()
    to_prev.start()
    c_next.start()
    c_prev.start()

    windowed = []
    for s in range(subs):
        relative = cmap[0, s : s + 1, :] - CPS * (me * subs + s) + CPS
        relative = jnp.where(relative < 0, relative + nc, relative)
        relative = jnp.where(relative >= nc, relative - nc, relative) + CPS * s
        pmax = relative.shape[1]
        spots = lax.broadcasted_iota(jnp.int32, (rows_w, pmax), 0)
        slots = lax.broadcasted_iota(jnp.int32, (rows_w, pmax), 1)
        hit = (spots == relative) & (slots < counts[:, s : s + 1])
        table = hit.astype(F32).astype(BF16)
        both = [dot(table, basis[0, s, c]) for c in range(2)]
        windowed.append(jnp.concatenate(both, axis=0))

    rows = lax.broadcasted_iota(jnp.int32, (nc, n * rows_w), 0)
    cols = lax.broadcasted_iota(jnp.int32, (nc, n * rows_w), 1)
    place = (cols // rows_w) * rows_own - CPS + lax.rem(cols, rows_w)
    place = jnp.where(place < 0, place + nc, place)
    place = jnp.where(place >= nc, place - nc, place)
    within = lax.rem(cols, rows_w) < rows_own + 2 * CPS
    pick = ((rows == place) & within).astype(F32).astype(BF16)

    load_vals.wait()
    load_kinv.wait()

    def combine(k_cols, real, imag):
        lhs = jnp.concatenate(k_cols, axis=1)
        rhs_real = jnp.concatenate([real, -imag], axis=0)
        rhs_imag = jnp.concatenate([imag, real], axis=0)
        return dot(lhs, rhs_real), dot(lhs, rhs_imag)

    def window_part(table, real, imag):
        high = table.astype(BF16)
        both_real, both_imag = dot(high, real), dot(high, imag)
        return (
            both_real[:rows_w] - both_imag[rows_w:],
            both_imag[:rows_w] + both_real[rows_w:],
        )

    w_real = jnp.zeros((rows_w, width), F32)
    w_imag = jnp.zeros((rows_w, width), F32)
    for s in range(subs):
        real, imag = vals[s, 0, shared:], vals[s, 1, shared:]
        part = window_part(windowed[s][:, shared:], real, imag)
        w_real, w_imag = w_real + part[0], w_imag + part[1]
        got = combine([kin[s, 0, :, shared:], kin[s, 1, :, shared:]], real, imag)
        acc[s, 0], acc[s, 1] = got

    to_next.wait_recv()
    to_prev.wait_recv()

    @pl.when(has_below)
    def _():
        to_above.wait_recv()

    @pl.when(has_above)
    def _():
        to_below.wait_recv()

    low = jnp.where(has_below, 0.5, 1.0).astype(F32)
    high = jnp.where(has_above, 0.5, 1.0).astype(F32)
    for s in range(subs):
        for c in range(2):
            own = [vals[s, c, IF * i : IF * (i + 1)].astype(F32) for i in range(4)]
            left = fprev[c] if s == 0 else vals[s - 1, c, IF : 2 * IF]
            right = fnext[c] if s == subs - 1 else vals[s + 1, c, 0:IF]
            zero = jnp.zeros((IF, width), F32)
            under = jnp.where(has_below, below[s, c].astype(F32), zero)
            over = jnp.where(has_above, above[s, c].astype(F32), zero)
            wt[s, c, 0:IF] = (0.5 * own[0] + 0.5 * left.astype(F32)).astype(BF16)
            wt[s, c, IF : 2 * IF] = (0.5 * own[1] + 0.5 * right.astype(F32)).astype(BF16)
            wt[s, c, 2 * IF : 3 * IF] = (low * own[2] + 0.5 * under).astype(BF16)
            wt[s, c, 3 * IF : 4 * IF] = (high * own[3] + 0.5 * over).astype(BF16)
        part = window_part(windowed[s][:, :shared], wt[s, 0], wt[s, 1])
        w_real, w_imag = w_real + part[0], w_imag + part[1]

    gather[me, 0] = w_real.astype(BF16)
    gather[me, 1] = w_imag.astype(BF16)

    def share(slot, where, i):
        return pltpu.make_async_remote_copy(
            src_ref=gather.at[slot], dst_ref=gather.at[slot],
            send_sem=ag_send.at[i], recv_sem=ag_recv.at[slot],
            device_id={"sub": where}, device_id_type=MESH,
        )

    def across(k):
        return share(me, lax.rem(chip + k, chips) * 2 + core, k)

    def source(k):
        return lax.rem(chip + chips - k, chips) * 2 + core

    def relay(k):
        return share(source(k), sib, chips + k)

    repeat(1, chips, lambda k: across(k).start())
    share(me, sib, 0).start()

    c_next.wait_recv()
    c_prev.wait_recv()
    pieces = []
    for c in range(2):
        parts = [cprev[0, c, rows_own - CPS :], coarse[0, c], cnext[0, c, :CPS]]
        extra = rows_w - rows_own - 2 * CPS
        if extra:
            parts.append(jnp.zeros((extra, nc), F32))
        pieces.extend(split(jnp.concatenate(parts, axis=0)))
    coarse_ext = dot(jnp.concatenate(pieces, axis=0), pick).astype(BF16)
    columns = [w.astype(BF16).T for w in windowed]

    def forward(k):
        share(source(k), sib, k).wait_recv()
        relay(k).start()

    for s in range(subs):
        got = combine([kin[s, 0, :, :shared], kin[s, 1, :, :shared]], wt[s, 0], wt[s, 1])
        acc[s, 0] += got[0]
        acc[s, 1] += got[1]

    repeat(1, chips, forward)
    repeat(0, chips, lambda k: share(lax.rem(chip + k, chips) * 2 + 1 - core, sib, 0).wait_recv())

    all_real = gather[:, 0].reshape(n * rows_w, width)
    all_imag = gather[:, 1].reshape(n * rows_w, width)
    by_real, by_imag = dot(coarse_ext, all_real), dot(coarse_ext, all_imag)

    def whole(x, i):
        return x[2 * i * rows_w : (2 * i + 1) * rows_w] + x[(2 * i + 1) * rows_w : (2 * i + 2) * rows_w]

    solved_real = whole(by_real, 0) - whole(by_imag, 1)
    solved_imag = whole(by_imag, 0) + whole(by_real, 1)
    real_high, real_low = split(solved_real)
    imag_high, imag_low = split(solved_imag)
    rhs_real = jnp.concatenate([real_high, -imag_high, real_low, -imag_low], axis=0)
    rhs_imag = jnp.concatenate([imag_high, real_high, imag_low, real_low], axis=0)
    for s in range(subs):
        lhs = jnp.concatenate([columns[s], columns[s]], axis=1)
        out[0, s, 0] = (acc[s, 0] + dot(lhs, rhs_real)).astype(BF16)
        out[0, s, 1] = (acc[s, 1] + dot(lhs, rhs_imag)).astype(BF16)

    to_next.wait_send()
    to_prev.wait_send()

    @pl.when(has_above)
    def _():
        to_above.wait_send()

    @pl.when(has_below)
    def _():
        to_below.wait_send()

    c_next.wait_send()
    c_prev.wait_send()
    share(me, sib, 0).wait_send()
    repeat(1, chips, lambda k: across(k).wait_send())
    repeat(1, chips, lambda k: relay(k).wait_send())


def per_device(n, groups, resid, kinv, basis, counts, coarse_map, coarse_inv):
    _, subs, _, order, width = resid.shape
    rows_w = -(-(CPS * (subs + 2)) // 16) * 16
    vmem = pl.BlockSpec(memory_space=pltpu.VMEM)
    hbm = pl.BlockSpec(memory_space=pltpu.HBM)
    dma = pltpu.SemaphoreType.DMA
    return pl.pallas_call(
        functools.partial(kernel, n, groups),
        out_shape=pltpu.VMEM(resid.shape, BF16),
        in_specs=[hbm] * 6,
        out_specs=vmem,
        scratch_shapes=[
            pltpu.VMEM(basis.shape, BF16),
            pltpu.VMEM(counts.shape, jnp.int32),
            pltpu.VMEM(coarse_map.shape, jnp.int32),
            pltpu.VMEM(coarse_inv.shape, F32),
            pltpu.VMEM(resid.shape[1:], BF16),
            pltpu.VMEM(kinv.shape[1:], BF16),
            pltpu.VMEM((subs, 2, IF, width), BF16),
            pltpu.VMEM((subs, 2, IF, width), BF16),
            pltpu.VMEM((2, IF, width), BF16),
            pltpu.VMEM((2, IF, width), BF16),
            pltpu.VMEM(coarse_inv.shape, F32),
            pltpu.VMEM(coarse_inv.shape, F32),
            pltpu.VMEM((n, 2, rows_w, width), BF16),
            pltpu.VMEM((subs, 2, 4 * IF, width), BF16),
            pltpu.VMEM((subs, 2, order, width), F32),
            dma((6,)), dma((6,)), dma((6,)), dma((n,)), dma((n,)),
        ],
        compiler_params=pltpu.CompilerParams(collective_id=0, has_side_effects=True),
    )(resid, kinv, basis, counts, coarse_map, coarse_inv)


def solution(mesh):
    return jax.shard_map(
        functools.partial(per_device, mesh.shape["sub"], mesh.shape["grp"]),
        mesh=mesh,
        in_specs=(
            P("grp", "sub", None, None, None),
            P("grp", "sub", None, None, None),
            P("grp", "sub", None, None, None),
            P("grp", "sub"),
            P("grp", "sub", None),
            P("grp", None, "sub", None),
        ),
        out_specs=P("grp", "sub", None, None, None),
        check_vma=False,
    )
```
